32 devices in a mesh: strip: 2 (over y), col: 4 (over z), row: 4 (over x, core).
Axes of the slice: x: 2, y: 2, z: 4, core: 2. Of those that a mesh axis runs over, the one named last changes fastest.
Arguments:
- left_features: bfloat16 [64, 2048, 128], P(('strip', 'row'), 'col'), parts along dimension 0, may hold values from -6 to 6
- right_features: bfloat16 [64, 2048, 128], P(('strip', 'row'), 'col'), parts along dimension 0, may hold values from -6 to 6
- conv_first: bfloat16 [3, 3, 256, 256], replicated, may hold values from -0.125 to 0.125
- conv_second: bfloat16 [3, 3, 256, 256], replicated, may hold values from -0.125 to 0.125
Outputs:
- cost_field: bfloat16 [64, 2048, 256], P(('strip', 'row'), 'col'), parts along dimension 0
The draws below stay inside these ranges and needn't reach their ends.
There are 2 independent parts, one for each index of `strip`. The reference program is written for one: setup_inputs(seed, part) draws one part's arguments, and reference() takes and returns one part's arrays. A program takes and returns all parts, laid end to end along the dimension named above; an argument that names none is the same for every part. Nothing has to cross between parts.
All inputs are finite; a program needn't handle non-finite values.
Results may differ from the reference program's by a relative error of at most 0.0058.
Values may be sent and summed in bfloat16 or wider, within the bound.
A program may use at most 128 MiB of HBM per device.

```python
import jax
import jax.numpy as jnp
from jax import lax

C = 128
DISP = 256
H = 32
W = 2048


def shard_levels(key, dims, pieces, low, high):
    gain = 1.0
    for position, shards_of in pieces:
        steps = jax.random.uniform(jax.random.fold_in(jax.random.fold_in(key, 6), position), (shards_of,), jnp.float32, low / len(pieces), high / len(pieces))
        gain = gain * jnp.repeat(jnp.exp(steps), dims[position] // shards_of).reshape((-1,) + (1,) * (len(dims) - 1 - position))
    return gain


def gaussian(rng, shape, scale, most, split=(), dtype=jnp.bfloat16):
    values = jax.random.normal(rng, shape, jnp.float32) * scale
    if len(split) > 0:
        values = shard_levels(rng, shape, split, -0.22, 0.18) * values
    return jnp.clip(values, min=-most, max=most).astype(dtype)


def setup_inputs(seed: int = 0, part: int = 0) -> dict:
    splits = jax.random.split(jax.random.key(seed), 5)
    part_splits = jax.random.split(jax.random.fold_in(splits[4], part), 5)
    return {
        "left_features": gaussian(part_splits[0], (H, W, C), 1.0, 6.0, ((0, 4), (1, 4))),
        "right_features": gaussian(part_splits[1], (H, W, C), 1.0, 6.0, ((0, 4), (1, 4))),
        "conv_first": gaussian(splits[2], (3, 3, DISP, DISP), (9 * DISP) ** -0.5, 0.125),
        "conv_second": gaussian(splits[3], (3, 3, DISP, DISP), (9 * DISP) ** -0.5, 0.125),
    }


def correlate(left_part, extended, disparities, chan_count):
    row_count, col_count = (left_part.shape[0], left_part.shape[1])
    block_count = col_count // disparities
    left_blocks = left_part.astype(jnp.float32).reshape(row_count, block_count, disparities, chan_count)
    right_blocks = extended.astype(jnp.float32).reshape(row_count, block_count + 1, disparities, chan_count)
    windows = jnp.concatenate((right_blocks[:, :-1], right_blocks[:, 1:]), axis=2)
    scores = jnp.einsum('rjwc,rjvc->rjwv', left_blocks, windows, precision=lax.Precision.HIGHEST)
    scores = scores * (1.0 / jnp.sqrt(jnp.float32(chan_count)))
    flat_scores = scores.reshape(row_count, block_count, disparities * 2 * disparities)
    flat_scores = jnp.pad(flat_scores, ((0, 0), (0, 0), (0, disparities)))
    skewed = flat_scores.reshape(row_count, block_count, disparities, 2 * disparities + 1)
    banded = skewed[..., 1:disparities + 1][..., ::-1]
    return banded.reshape(row_count, col_count, disparities).astype(jnp.bfloat16)

def convolve_same(image, kernel):
    result = lax.conv_general_dilated(image.astype(jnp.float32)[None], kernel.astype(jnp.float32), (1, 1), 'SAME', dimension_numbers=('NHWC', 'HWIO', 'NHWC'), precision=lax.Precision.HIGHEST)
    return result[0]

def reference(left_features, right_features, conv_first, conv_second):
    zero_cols = jnp.zeros((H, DISP, C), jnp.bfloat16)
    extended = jnp.concatenate((zero_cols, right_features), axis=1)

    def one_row(pair):
        return correlate(pair[0][None], pair[1][None], DISP, C)[0]
    volume = lax.map(one_row, (left_features, extended))
    hidden = jax.nn.relu(convolve_same(volume, conv_first)).astype(jnp.bfloat16)
    return jax.nn.relu(convolve_same(hidden, conv_second)).astype(jnp.bfloat16)
```

```python
import functools

import jax
import jax.numpy as jnp
from jax import lax
from jax.experimental import pallas as pl
from jax.experimental.pallas import tpu as pltpu
from jax.sharding import PartitionSpec as P

MESH = pl.DeviceIdType.MESH
F32 = jnp.float32
BF16 = jnp.bfloat16
E = 16
G = 32
LANES = 128


def kernel(
    ncol, nrow, left, right, w1_hbm, w2_hbm, out,
    rext, lext, rrev, vol3, hid3, vrim, hrim, w1, w2, lsem, ssem, rsem,
):
    rows, width, chans = left.shape
    disp = w2_hbm.shape[1]
    col = lax.axis_index("col")
    row = lax.axis_index("row")
    has_l, has_r = col > 0, col < ncol - 1
    has_u, has_d = row > 0, row < nrow - 1
    to_l, to_r = {"col": col - 1}, {"col": col + 1}
    to_u, to_d = {"row": row - 1}, {"row": row + 1}
    halo = disp + E
    window = disp + LANES

    barrier = pltpu.get_barrier_semaphore()
    for has, to in ((has_l, to_l), (has_r, to_r), (has_u, to_u), (has_d, to_d)):
        @pl.when(has)
        def _():
            pl.semaphore_signal(barrier, inc=1, device_id=to, device_id_type=MESH)

    own = [
        pltpu.make_async_copy(right, rext.at[:, halo : halo + width], lsem.at[0]),
        pltpu.make_async_copy(left, lext.at[:, E : E + width], lsem.at[1]),
        pltpu.make_async_copy(w1_hbm, w1, lsem.at[2]),
        pltpu.make_async_copy(w2_hbm, w2, lsem.at[3]),
    ]
    for copy in own:
        copy.start()

    def clear(ref, *at):
        ref[at] = jnp.zeros(ref.at[at].shape, BF16)

    every = slice(0, rows)

    @pl.when(jnp.logical_not(has_l))
    def _():
        clear(rext, every, slice(0, halo))
        clear(lext, every, slice(0, E))

    @pl.when(jnp.logical_not(has_r))
    def _():
        clear(rext, every, slice(halo + width, halo + width + E))
        clear(lext, every, slice(E + width, 2 * E + width))

    @pl.when(jnp.logical_not(has_u))
    def _():
        clear(vrim, 0)
        clear(hrim, 0)

    @pl.when(jnp.logical_not(has_d))
    def _():
        clear(vrim, 1)
        clear(hrim, 1)

    peers = sum(has.astype(jnp.int32) for has in (has_l, has_r, has_u, has_d))
    pl.semaphore_wait(barrier, peers)

    counter = [0]

    def remote(src, dst, to):
        at = counter[0]
        counter[0] += 1
        return pltpu.make_async_remote_copy(
            src_ref=src, dst_ref=dst, send_sem=ssem.at[at], recv_sem=rsem.at[at],
            device_id=to, device_id_type=MESH,
        )

    def start(has, copies):
        @pl.when(has)
        def _():
            for copy in copies:
                copy.start()

    def recv(has, copies):
        @pl.when(has)
        def _():
            for copy in copies:
                copy.wait_recv()

    def sent(has, copies):
        @pl.when(has)
        def _():
            for copy in copies:
                copy.wait_send()

    b0, b1, b2, b3, b4 = -E, disp // 4, disp // 2, disp, width + E
    vcols = [(b3, b4), (b2, b3), (b1, b2), (b0, b1)]
    hcols = [(b3 + E, b4), (b2 + E, b3 + E), (b1 + E, b2 + E), (b0, b1 + E)]
    ocols = [(b3 + 2 * E, width), (b2 + 2 * E, b3 + 2 * E), (b1 + 2 * E, b2 + 2 * E), (0, b1 + 2 * E)]
    SA, SB, SC, SD = range(4)

    def halo_part(first, last, r0, r1):
        return remote(
            right.at[r0:r1, width + first : width + last],
            rext.at[r0:r1, halo + first : halo + last], to_r,
        )

    edge_l = [
        remote(left.at[:, 0:E], lext.at[:, E + width : 2 * E + width], to_l),
        remote(right.at[:, 0:E], rext.at[:, halo + width : halo + width + E], to_l),
    ]
    near = [halo_part(b2 - disp, 0, 0, rows)]
    mid = [halo_part(b1 - disp, b2 - disp, 0, rows)]
    edge_r = [remote(left.at[:, width - E : width], lext.at[:, 0:E], to_r)]
    far = [halo_part(b0 - disp, b1 - disp, r, r + 2) for r in (0, rows - 2)]
    far_rest = [halo_part(b0 - disp, b1 - disp, 2, rows - 2)]

    def rim(ref3, ref, cols):
        l, h = cols[0] + G, cols[1] + G
        mid_lanes = slice(disp, 2 * disp)
        up = remote(ref3.at[1, l:h, mid_lanes], ref.at[1, l:h], to_u)
        down = remote(ref3.at[rows, l:h, mid_lanes], ref.at[0, l:h], to_d)
        return [up], [down]

    vrims = [rim(vol3, vrim, c) for c in vcols]
    hrims = [rim(hid3, hrim, c) for c in hcols]

    start(has_l, edge_l)
    start(has_r, near + mid + edge_r)
    start(has_r, far + far_rest)

    scale = 1.0 / jnp.sqrt(F32(chans))

    def store3(ref3, r, first, value):
        n = value.shape[0]
        for b in range(3):
            at = first + G + 1 - b
            ref3[r, at : at + n, b * disp : (b + 1) * disp] = value

    def correlate(r, first, count):
        at = width + E - first - count
        scores = lax.dot_general(
            lext[r, first + E : first + E + count, :],
            rrev[r, at : at + window, :],
            (((1,), (1,)), ((), ())),
            preferred_element_type=F32,
        )
        i = lax.broadcasted_iota(jnp.int32, (count, LANES), 0)
        j = lax.broadcasted_iota(jnp.int32, (count, LANES), 1)
        ahead = i + j >= count - 1
        blocks = [scores[:, k : k + LANES] for k in range(0, window, LANES)]
        turned = [
            pltpu.roll(jnp.where(ahead, p, q), LANES + 1 - count, 1, stride=1, stride_axis=0)
            for p, q in zip(blocks, blocks[1:])
        ]
        store3(vol3, r + 1, first, (jnp.concatenate(turned, axis=1) * scale).astype(BF16))

    def flip(r, first, count):
        i = lax.broadcasted_iota(jnp.int32, (count, count), 0)
        j = lax.broadcasted_iota(jnp.int32, (count, count), 1)
        turn = jnp.where(i + j == count - 1, 1.0, 0.0).astype(BF16)
        pair = jnp.concatenate([rext[r + k, halo + first : halo + first + count, :] for k in range(2)], axis=1)
        piece = jnp.dot(turn, pair, preferred_element_type=F32).astype(BF16)
        at = width + E - first - count
        for k in range(2):
            rrev[r + k, at : at + count, :] = piece[:, k * chans : (k + 1) * chans]

    def tiles(cols):
        units = (cols[1] - cols[0]) // E
        n = -(-units * E // LANES)
        ends = [cols[0] + E * (units * k // n) for k in range(n + 1)]
        return [(p, q - p) for p, q in zip(ends, ends[1:])]

    def correlate_all(seg, per):
        @pl.loop(0, rows // per)
        def _(p):
            for k in range(per):
                for first, count in tiles(vcols[seg]):
                    correlate(p * per + k, first, count)

    def correlate_rows(seg, rs):
        for r in rs:
            for first, count in tiles(vcols[seg]):
                correlate(r, first, count)

    def send_rims(rims, seg):
        start(has_u, rims[seg][0])
        start(has_d, rims[seg][1])

    def take_rims(rims, ref, ref3, cols, seg):
        recv(has_d, rims[seg][0])
        recv(has_u, rims[seg][1])
        l, h = cols[seg]
        store3(ref3, 0, l, ref[0, l + G : h + G, :])
        store3(ref3, rows + 1, l, ref[1, l + G : h + G, :])

    def gathered(ref3, groups, l, h):
        return jnp.concatenate(
            [
                jnp.concatenate(
                    [ref3[pl.ds(g + a, n), l + G : h + G, :].reshape(n * (h - l), 3 * disp) for g, n in groups], axis=0
                )
                for a in range(3)
            ],
            axis=1,
        )

    def conv1(seg, groups):
        l, h = hcols[seg]
        size = h - l
        acc = jnp.dot(gathered(vol3, groups, l, h), w1[...], preferred_element_type=F32)
        masked = l < 0 or h > width
        if masked:
            at = col * width + l + lax.broadcasted_iota(jnp.int32, (size, 1), 0)
            inside = (at >= 0) & (at < ncol * width)
        k = 0
        for g, n in groups:
            for r in range(n):
                value = jnp.maximum(acc[k * size : (k + 1) * size], 0.0)
                if masked:
                    value = jnp.where(inside, value, 0.0)
                store3(hid3, g + r + 1, l, value.astype(BF16))
                k += 1

    def conv2(seg, groups):
        l, h = ocols[seg]
        size = h - l
        acc = jnp.dot(gathered(hid3, groups, l, h), w2[...], preferred_element_type=F32)
        acc = jnp.maximum(acc, 0.0).astype(BF16)
        k = 0
        for g, n in groups:
            out[pl.ds(g, n), l:h, :] = acc[k * size : (k + n) * size].reshape(n, size, disp)
            k += n

    half = rows // 2
    steps = rows // 4

    def inner(i):
        return [(half - 2 - 2 * i, 2), (half + 2 * i, 2)]

    def by_parts(conv, seg, last):
        @pl.loop(0, steps)
        def _(i):
            @pl.when(i == steps - 1)
            def _():
                last()
            conv(seg, inner(i))

    def take_v(seg):
        take_rims(vrims, vrim, vol3, vcols, seg)

    def take_h(seg):
        take_rims(hrims, hrim, hid3, hcols, seg)

    whole = [(0, rows)]

    def flip_all(cols, rs):
        for r in rs:
            for first, count in tiles(cols):
                flip(r, first, count)

    pairs = range(0, rows, 2)
    own[0].wait()
    own[1].wait()
    recv(has_r, edge_l)

    @pl.loop(0, half)
    def _(p):
        flip_all((0, width + E), [2 * p])

    correlate_all(SA, 2)
    send_rims(vrims, SA)
    own[2].wait()
    by_parts(conv1, SA, lambda: take_v(SA))
    send_rims(hrims, SA)
    own[3].wait()
    by_parts(conv2, SA, lambda: take_h(SA))
    recv(has_l, near)
    flip_all((b2 - disp, 0), pairs)
    correlate_all(SB, 4)
    send_rims(vrims, SB)
    take_v(SB)
    conv1(SB, whole)
    send_rims(hrims, SB)
    recv(has_l, mid)
    flip_all((b1 - disp, b2 - disp), pairs)
    correlate_all(SC, 4)
    send_rims(vrims, SC)
    take_h(SB)
    conv2(SB, whole)
    take_v(SC)
    conv1(SC, whole)
    send_rims(hrims, SC)
    ends = [0, 1, rows - 2, rows - 1]
    recv(has_l, edge_r + far)
    flip_all((b0 - disp, b1 - disp), [0, rows - 2])
    correlate_rows(SD, ends)
    send_rims(vrims, SD)
    take_h(SC)
    conv2(SC, whole)
    take_v(SD)
    conv1(SD, [(0, 1), (rows - 1, 1)])
    send_rims(hrims, SD)
    recv(has_l, far_rest)
    flip_all((b0 - disp, b1 - disp), range(2, rows - 2, 2))
    correlate_rows(SD, range(2, rows - 2))
    conv1(SD, [(1, rows - 2)])
    take_h(SD)
    conv2(SD, whole)

    sent(has_l, edge_l)
    sent(has_r, near + mid + edge_r + far + far_rest)
    for rims in (vrims, hrims):
        for up, down in rims:
            sent(has_u, up)
            sent(has_d, down)


def local(ncol, nrow, left, right, w1, w2):
    rows, width, chans = left.shape
    disp = w1.shape[2]
    outs = w1.shape[3]
    w1 = w1.reshape(-1, outs)
    w2 = w2.reshape(-1, outs)
    span = width + disp + 2 * E + LANES
    wide = width + 2 * G
    hbm = pl.BlockSpec(memory_space=pl.ANY)
    copies = 24
    return pl.pallas_call(
        functools.partial(fixed, ncol, nrow),
        out_shape=pltpu.VMEM((rows, width, outs), BF16),
        in_specs=[hbm] * 4,
        out_specs=pl.BlockSpec(memory_space=pltpu.VMEM),
        scratch_shapes=[
            pltpu.VMEM((rows, width + disp + 2 * E, chans), BF16),
            pltpu.VMEM((rows, width + 2 * E, chans), BF16),
            pltpu.VMEM((rows, span, chans), BF16),
            pltpu.VMEM((rows + 2, wide, 3 * disp), BF16),
            pltpu.VMEM((rows + 2, wide, 3 * outs), BF16),
            pltpu.VMEM((2, wide, disp), BF16),
            pltpu.VMEM((2, wide, outs), BF16),
            pltpu.VMEM(w1.shape, BF16),
            pltpu.VMEM(w2.shape, BF16),
            pltpu.SemaphoreType.DMA((4,)),
            pltpu.SemaphoreType.DMA((copies,)),
            pltpu.SemaphoreType.DMA((copies,)),
        ],
        compiler_params=pltpu.CompilerParams(
            collective_id=0, has_side_effects=True, vmem_limit_bytes=67_043_328 - 2 * rows * width * outs - 2**18
        ),
    )(left, right, w1, w2)


def fixed(ncol, nrow, *refs):
    kernel(ncol, nrow, *refs)


def solution(mesh):
    in_specs = (P(("strip", "row"), "col", None), P(("strip", "row"), "col", None), P(), P())
    out_specs = P(("strip", "row"), "col", None)
    return jax.shard_map(
        functools.partial(local, mesh.shape["col"], mesh.shape["row"]),
        mesh=mesh, in_specs=in_specs, out_specs=out_specs, check_vma=False,
    )
```

```python
import functools

import jax
import jax.numpy as jnp
from jax import lax
from jax.experimental import pallas as pl
from jax.experimental.pallas import tpu as pltpu
from jax.sharding import PartitionSpec as P

MESH = pl.DeviceIdType.MESH
F32 = jnp.float32
BF16 = jnp.bfloat16
E = 16
G = 32
LANES = 128


def kernel(
    ncol, nrow, left, right, w1_hbm, w2_hbm, out,
    rext, lext, rrev, vmid, vout, hmid, hout, w1, w2, lsem, ssem, rsem,
):
    rows, width, chans = left.shape
    disp = w2_hbm.shape[1]
    col = lax.axis_index("col")
    row = lax.axis_index("row")
    has_l, has_r = col > 0, col < ncol - 1
    has_u, has_d = row > 0, row < nrow - 1
    to_l, to_r = {"col": col - 1}, {"col": col + 1}
    to_u, to_d = {"row": row - 1}, {"row": row + 1}
    halo = disp + E
    window = disp + LANES

    barrier = pltpu.get_barrier_semaphore()
    for has, to in ((has_l, to_l), (has_r, to_r), (has_u, to_u), (has_d, to_d)):
        @pl.when(has)
        def _():
            pl.semaphore_signal(barrier, inc=1, device_id=to, device_id_type=MESH)

    own = [
        pltpu.make_async_copy(right, rext.at[:, halo : halo + width], lsem.at[0]),
        pltpu.make_async_copy(left, lext.at[:, E : E + width], lsem.at[1]),
        pltpu.make_async_copy(w1_hbm, w1, lsem.at[2]),
        pltpu.make_async_copy(w2_hbm, w2, lsem.at[3]),
    ]
    for copy in own:
        copy.start()

    def clear(ref, *at):
        ref[at] = jnp.zeros(ref.at[at].shape, BF16)

    every = slice(0, rows)

    @pl.when(jnp.logical_not(has_l))
    def _():
        clear(rext, every, slice(0, halo))
        clear(lext, every, slice(0, E))

    @pl.when(jnp.logical_not(has_r))
    def _():
        clear(rext, every, slice(halo + width, halo + width + E))
        clear(lext, every, slice(E + width, 2 * E + width))

    @pl.when(jnp.logical_not(has_u))
    def _():
        clear(vmid, slice(0, 2))

    @pl.when(jnp.logical_not(has_d))
    def _():
        clear(vmid, slice(rows + 2, rows + 4))

    peers = sum(has.astype(jnp.int32) for has in (has_l, has_r, has_u, has_d))

    counter = [0]

    def remote(src, dst, to):
        at = counter[0]
        counter[0] += 1
        return pltpu.make_async_remote_copy(
            src_ref=src, dst_ref=dst, send_sem=ssem.at[at], recv_sem=rsem.at[at],
            device_id=to, device_id_type=MESH,
        )

    def start(has, copies):
        @pl.when(has)
        def _():
            for copy in copies:
                copy.start()

    def recv(has, copies):
        @pl.when(has)
        def _():
            for copy in copies:
                copy.wait_recv()

    def sent(has, copies):
        @pl.when(has)
        def _():
            for copy in copies:
                copy.wait_send()

    b0, b1, b2, b3, b4 = -E, 5 * E, 11 * E, disp, width - E
    vcols = [[(b3, b4)], [(b2, b3), (b4, width + E)], [(b1, b2)], [(b0, b1)]]
    hcols = [[(b3 + E, b4 - E)], [(b2 + E, b3 + E), (b4 - E, width + E)], [(b1 + E, b2 + E)], [(b0, b1 + E)]]
    ocols = [
        [(b3 + 2 * E, b4 - 2 * E)],
        [(b2 + 2 * E, b3 + 2 * E), (b4 - 2 * E, width)],
        [(b1 + 2 * E, b2 + 2 * E)],
        [(0, b1 + 2 * E)],
    ]
    SA, SB, SC, SD = range(4)

    def halo_part(first, last, r0, r1):
        return remote(
            right.at[r0:r1, width + first : width + last],
            rext.at[r0:r1, halo + first : halo + last], to_r,
        )

    edge_l = [
        remote(left.at[:, 0:E], lext.at[:, E + width : 2 * E + width], to_l),
        remote(right.at[:, 0:E], rext.at[:, halo + width : halo + width + E], to_l),
    ]
    near = [halo_part(b2 - disp, 0, 0, rows)]
    mid = [halo_part(b1 - disp, b2 - disp, 0, rows)]
    edge_r = [remote(left.at[:, width - E : width], lext.at[:, 0:E], to_r)]
    far = [halo_part(b0 - disp, b1 - disp, r, r + 2) for r in (0, rows - 2)]
    far_rest = [halo_part(b0 - disp, b1 - disp, 2, rows - 2)]

    def rim(cols):
        ups, downs = [], []
        for c in cols:
            at = slice(c[0] + G, c[1] + G)
            ups.append(remote(vmid.at[2:4, at], vmid.at[rows + 2 : rows + 4, at], to_u))
            downs.append(remote(vmid.at[rows : rows + 2, at], vmid.at[0:2, at], to_d))
        return ups, downs

    rims = [rim(c) for c in vcols]

    once = (col >= 0).astype(jnp.int32)
    scale = 1.0 / jnp.sqrt(F32(chans))

    def spread(out_ref, r, first, value):
        n = value.shape[0]
        for b in (0, 1):
            at = first + G + 1 - 2 * b
            out_ref[r, at : at + n, b * disp : (b + 1) * disp] = value

    def store(mid_ref, out_ref, r, first, value):
        mid_ref[r, first + G : first + G + value.shape[0], :] = value
        spread(out_ref, r, first, value)

    def correlate(r, first, count):
        at = width + E - first - count
        scores = lax.dot_general(
            lext[r, first + E : first + E + count, :],
            rrev[r, at : at + window, :],
            (((1,), (1,)), ((), ())),
            preferred_element_type=F32,
        )
        i = lax.broadcasted_iota(jnp.int32, (count, LANES), 0)
        j = lax.broadcasted_iota(jnp.int32, (count, LANES), 1)
        ahead = i + j >= count - 1
        blocks = [scores[:, k : k + LANES] for k in range(0, window, LANES)]
        turned = [
            pltpu.roll(jnp.where(ahead, p, q), LANES + 1 - count, 1, stride=1, stride_axis=0)
            for p, q in zip(blocks, blocks[1:])
        ]
        store(vmid, vout, r + 2, first, (jnp.concatenate(turned, axis=1) * scale).astype(BF16))

    def flip(r, first, count):
        i = lax.broadcasted_iota(jnp.int32, (count, count), 0)
        j = lax.broadcasted_iota(jnp.int32, (count, count), 1)
        turn = jnp.where(i + j == count - 1, 1.0, 0.0).astype(BF16)
        pair = jnp.concatenate([rext[r + k, halo + first : halo + first + count, :] for k in range(2)], axis=1)
        piece = jnp.dot(turn, pair, preferred_element_type=F32).astype(BF16)
        at = width + E - first - count
        for k in range(2):
            rrev[r + k, at : at + count, :] = piece[:, k * chans : (k + 1) * chans]

    def tiles(cols):
        units = (cols[1] - cols[0]) // E
        n = -(-units * E // LANES)
        ends = [cols[0] + E * (units * k // n) for k in range(n + 1)]
        return [(p, q - p) for p, q in zip(ends, ends[1:])]

    def correlate_rows(seg, rs):
        for r in rs:
            for cols in vcols[seg]:
                for first, count in tiles(cols):
                    correlate(r, first, count)

    def correlate_loop(seg, first, n, per):
        @pl.loop(0, n // per)
        def _(p):
            correlate_rows(seg, [first + p * per + k for k in range(per)])

    def flip_rows(cols, rs):
        for r in rs:
            for first, count in tiles(cols):
                flip(r, first, count)

    def send_rims(seg):
        start(has_u, rims[seg][0])
        start(has_d, rims[seg][1])

    def take_rims(seg):
        recv(has_d, rims[seg][0])
        recv(has_u, rims[seg][1])
        for l, h in vcols[seg]:
            for r in (0, 1, rows + 2, rows + 3):
                spread(vout, r, l, vmid[r, l + G : h + G, :])

    def gathered(mid_ref, out_ref, shift, parts):
        taps = [(out_ref, slice(0, disp)), (mid_ref, slice(0, disp)), (out_ref, slice(disp, 2 * disp))]
        return jnp.concatenate(
            [
                jnp.concatenate(
                    [
                        ref[pl.ds(g + a + shift, n), l + G : h + G, lanes].reshape(n * (h - l), disp)
                        for g, n, (l, h) in parts
                    ],
                    axis=0,
                )
                for a in range(3)
                for ref, lanes in taps
            ],
            axis=1,
        )

    def apart(body):
        @pl.loop(0, once)
        def _(_):
            body()

    def shares(parts):
        total = sum(n * (h - l) for _, n, (l, h) in parts)
        first, second, done = [], [], 0
        for g, n, (l, h) in parts:
            take = min(n, max(0, round((total / 2 - done) / (h - l))))
            if take:
                first.append((g, take, (l, h)))
                done += take * (h - l)
            if take < n:
                second.append((g + take, n - take, (l, h)))
        return [p for p in (first, second) if p]

    def conv1(parts):
        @apart
        def _():
            for share in shares(parts):
                conv1_share(share)

    def conv2(parts):
        @apart
        def _():
            for share in shares(parts):
                conv2_share(share)

    def conv1_share(parts):
        acc = jnp.dot(gathered(vmid, vout, 1, parts), w1[...], preferred_element_type=F32)
        at = 0
        for g, n, (l, h) in parts:
            size = h - l
            masked = l < 0 or h > width
            if masked:
                x = col * width + l + lax.broadcasted_iota(jnp.int32, (size, 1), 0)
                inside = (x >= 0) & (x < ncol * width)
            for r in range(g, g + n):
                value = jnp.maximum(acc[at : at + size], 0.0)
                if masked:
                    value = jnp.where(inside, value, 0.0)
                if r < 0 or r >= rows:
                    value = jnp.where(has_u if r < 0 else has_d, value, 0.0)
                store(hmid, hout, r + 1, l, value.astype(BF16))
                at += size

    def conv2_share(parts):
        acc = jnp.dot(gathered(hmid, hout, 0, parts), w2[...], preferred_element_type=F32)
        acc = jnp.maximum(acc, 0.0).astype(BF16)
        at = 0
        for g, n, (l, h) in parts:
            size = n * (h - l)
            out[pl.ds(g, n), l:h, :] = acc[at : at + size].reshape(n, h - l, disp)
            at += size

    def parts_of(groups, cols):
        return [(g, n, c) for g, n in groups for c in cols]

    def hid_inner(seg):
        return parts_of([(1, rows - 2)], hcols[seg])

    def hid_outer(seg):
        return parts_of([(-1, 2), (rows - 1, 2)], hcols[seg])

    def out_inner(seg):
        return parts_of([(2, rows - 4)], ocols[seg])

    def out_outer(seg):
        return parts_of([(0, 2), (rows - 2, 2)], ocols[seg])

    outer_rows = [0, 1, rows - 2, rows - 1]
    pairs = range(0, rows, 2)
    pl.semaphore_wait(barrier, peers)
    start(has_l, edge_l)
    start(has_r, near + mid + edge_r + far + far_rest)
    own[0].wait()

    @pl.loop(0, rows // 2)
    def _(p):
        flip_rows((0, width), [2 * p])

    own[1].wait()

    @pl.loop(0, 2)
    def _(p):
        correlate_rows(SA, [(rows - 2) * p, (rows - 2) * p + 1])

    send_rims(SA)
    correlate_loop(SA, 2, rows - 4, 2)
    own[2].wait()
    conv1(hid_inner(SA))
    own[3].wait()
    conv2(out_inner(SA))

    recv(has_r, edge_l)
    recv(has_l, near)
    flip_rows((b2 - disp, 0), pairs)
    flip_rows((width, width + E), pairs)
    correlate_loop(SB, 0, rows, 4)
    send_rims(SB)
    take_rims(SA)
    conv1(hid_outer(SA) + hid_inner(SB))
    conv2(out_outer(SA) + out_inner(SB))

    recv(has_l, mid)
    flip_rows((b1 - disp, b2 - disp), pairs)
    correlate_loop(SC, 0, rows, 4)
    send_rims(SC)
    take_rims(SB)
    conv1(hid_outer(SB) + hid_inner(SC))
    conv2(out_outer(SB) + out_inner(SC))

    recv(has_l, edge_r + far)
    flip_rows((b0 - disp, b1 - disp), [0, rows - 2])
    correlate_rows(SD, outer_rows)
    send_rims(SD)
    recv(has_l, far_rest)
    flip_rows((b0 - disp, b1 - disp), range(2, rows - 2, 2))
    correlate_rows(SD, range(2, rows - 2))
    take_rims(SC)
    conv1(hid_outer(SC) + hid_inner(SD))
    conv2(out_outer(SC) + out_inner(SD))
    take_rims(SD)
    conv1(hid_outer(SD))
    conv2(out_outer(SD))

    sent(has_l, edge_l)
    sent(has_r, near + mid + edge_r + far + far_rest)
    for ups, downs in rims:
        sent(has_u, ups)
        sent(has_d, downs)


def local(ncol, nrow, left, right, w1, w2):
    rows, width, chans = left.shape
    disp = w1.shape[2]
    outs = w1.shape[3]
    w1 = w1.reshape(-1, outs)
    w2 = w2.reshape(-1, outs)
    span = width + disp + 2 * E + LANES
    wide = width + 2 * G
    hbm = pl.BlockSpec(memory_space=pl.ANY)
    copies = 18
    return pl.pallas_call(
        functools.partial(fixed, ncol, nrow),
        out_shape=pltpu.VMEM((rows, width, outs), BF16),
        in_specs=[hbm] * 4,
        out_specs=pl.BlockSpec(memory_space=pltpu.VMEM),
        scratch_shapes=[
            pltpu.VMEM((rows, width + disp + 2 * E, chans), BF16),
            pltpu.VMEM((rows, width + 2 * E, chans), BF16),
            pltpu.VMEM((rows, span, chans), BF16),
            pltpu.VMEM((rows + 4, wide, disp), BF16),
            pltpu.VMEM((rows + 4, wide, 2 * disp), BF16),
            pltpu.VMEM((rows + 2, wide, outs), BF16),
            pltpu.VMEM((rows + 2, wide, 2 * outs), BF16),
            pltpu.VMEM(w1.shape, BF16),
            pltpu.VMEM(w2.shape, BF16),
            pltpu.SemaphoreType.DMA((4,)),
            pltpu.SemaphoreType.DMA((copies,)),
            pltpu.SemaphoreType.DMA((copies,)),
        ],
        compiler_params=pltpu.CompilerParams(
            collective_id=0, has_side_effects=True, vmem_limit_bytes=67_043_328 - 2 * rows * width * outs - 2**18
        ),
    )(left, right, w1, w2)


def fixed(ncol, nrow, *refs):
    kernel(ncol, nrow, *refs)


def solution(mesh):
    in_specs = (P(("strip", "row"), "col", None), P(("strip", "row"), "col", None), P(), P())
    out_specs = P(("strip", "row"), "col", None)
    return jax.shard_map(
        functools.partial(local, mesh.shape["col"], mesh.shape["row"]),
        mesh=mesh, in_specs=in_specs, out_specs=out_specs, check_vma=False,
    )
```

```python
import functools

import jax
import jax.numpy as jnp
from jax import lax
from jax.experimental import pallas as pl
from jax.experimental.pallas import tpu as pltpu
from jax.sharding import PartitionSpec as P

MESH = pl.DeviceIdType.MESH
F32 = jnp.float32
BF16 = jnp.bfloat16
E = 16
G = 32
LANES = 128


def kernel(
    ncol, nrow, left, right, w1_hbm, w2_hbm, out,
    rext, lext, rrev, vmid, vout, hmid, hout, w1, w2, lsem, ssem, rsem,
):
    rows, width, chans = left.shape
    disp = w2_hbm.shape[1]
    col = lax.axis_index("col")
    row = lax.axis_index("row")
    has_l, has_r = col > 0, col < ncol - 1
    has_u, has_d = row > 0, row < nrow - 1
    to_l, to_r = {"col": col - 1}, {"col": col + 1}
    to_u, to_d = {"row": row - 1}, {"row": row + 1}
    halo = disp + E
    window = disp + LANES

    barrier = pltpu.get_barrier_semaphore()
    for has, to in ((has_l, to_l), (has_r, to_r), (has_u, to_u), (has_d, to_d)):
        @pl.when(has)
        def _():
            pl.semaphore_signal(barrier, inc=1, device_id=to, device_id_type=MESH)

    own = [
        pltpu.make_async_copy(right, rext.at[:, halo : halo + width], lsem.at[0]),
        pltpu.make_async_copy(left, lext.at[:, E : E + width], lsem.at[1]),
        pltpu.make_async_copy(w1_hbm, w1, lsem.at[2]),
        pltpu.make_async_copy(w2_hbm, w2, lsem.at[3]),
    ]
    for copy in own:
        copy.start()

    def clear(ref, *at):
        ref[at] = jnp.zeros(ref.at[at].shape, BF16)

    every = slice(0, rows)

    @pl.when(jnp.logical_not(has_l))
    def _():
        clear(rext, every, slice(0, halo))
        clear(lext, every, slice(0, E))

    @pl.when(jnp.logical_not(has_r))
    def _():
        clear(rext, every, slice(halo + width, halo + width + E))
        clear(lext, every, slice(E + width, 2 * E + width))

    @pl.when(jnp.logical_not(has_u))
    def _():
        clear(vmid, slice(0, 2))

    @pl.when(jnp.logical_not(has_d))
    def _():
        clear(vmid, slice(rows + 2, rows + 4))

    peers = sum(has.astype(jnp.int32) for has in (has_l, has_r, has_u, has_d))

    counter = [0]

    def remote(src, dst, to):
        at = counter[0]
        counter[0] += 1
        return pltpu.make_async_remote_copy(
            src_ref=src, dst_ref=dst, send_sem=ssem.at[at], recv_sem=rsem.at[at],
            device_id=to, device_id_type=MESH,
        )

    def start(has, copies):
        @pl.when(has)
        def _():
            for copy in copies:
                copy.start()

    def recv(has, copies):
        @pl.when(has)
        def _():
            for copy in copies:
                copy.wait_recv()

    def sent(has, copies):
        @pl.when(has)
        def _():
            for copy in copies:
                copy.wait_send()

    b0, b1, b2, b3, b4 = -E, 4 * E, 12 * E, disp, width - E
    vcols = [[(b3, b4)], [(b2, b3), (b4, width + E)], [(b1, b2)], [(b0, b1)]]
    hcols = [[(b3 + E, b4 - E)], [(b2 + E, b3 + E), (b4 - E, width + E)], [(b1 + E, b2 + E)], [(b0, b1 + E)]]
    ocols = [
        [(b3 + 2 * E, b4 - 2 * E)],
        [(b2 + 2 * E, b3 + 2 * E), (b4 - 2 * E, width)],
        [(b1 + 2 * E, b2 + 2 * E)],
        [(0, b1 + 2 * E)],
    ]
    SA, SB, SC, SD = range(4)

    def halo_part(first, last, r0, r1):
        return remote(
            right.at[r0:r1, width + first : width + last],
            rext.at[r0:r1, halo + first : halo + last], to_r,
        )

    edge_l = [
        remote(left.at[:, 0:E], lext.at[:, E + width : 2 * E + width], to_l),
        remote(right.at[:, 0:E], rext.at[:, halo + width : halo + width + E], to_l),
    ]
    near = [halo_part(b2 - disp, 0, 0, rows)]
    mid = [halo_part(b1 - disp, b2 - disp, 0, rows)]
    edge_r = [remote(left.at[:, width - E : width], lext.at[:, 0:E], to_r)]
    far = [halo_part(b0 - disp, b1 - disp, r, r + 2) for r in (0, rows - 2)]
    far_rest = [halo_part(b0 - disp, b1 - disp, 2, rows - 2)]

    def rim(cols):
        ups, downs = [], []
        for c in cols:
            at = slice(c[0] + G, c[1] + G)
            ups.append(remote(vmid.at[2:4, at], vmid.at[rows + 2 : rows + 4, at], to_u))
            downs.append(remote(vmid.at[rows : rows + 2, at], vmid.at[0:2, at], to_d))
        return ups, downs

    rims = [rim(c) for c in vcols]

    once = (col >= 0).astype(jnp.int32)
    scale = 1.0 / jnp.sqrt(F32(chans))

    def spread(out_ref, r, first, value):
        n = value.shape[0]
        for b in (0, 1):
            at = first + G + 1 - 2 * b
            out_ref[r, at : at + n, b * disp : (b + 1) * disp] = value

    def store(mid_ref, out_ref, r, first, value):
        mid_ref[r, first + G : first + G + value.shape[0], :] = value
        spread(out_ref, r, first, value)

    def correlate(r, first, count):
        at = width + E - first - count
        scores = lax.dot_general(
            lext[r, first + E : first + E + count, :],
            rrev[r, at : at + window, :],
            (((1,), (1,)), ((), ())),
            preferred_element_type=F32,
        )
        i = lax.broadcasted_iota(jnp.int32, (count, LANES), 0)
        j = lax.broadcasted_iota(jnp.int32, (count, LANES), 1)
        ahead = i + j >= count - 1
        blocks = [scores[:, k : k + LANES] for k in range(0, window, LANES)]
        turned = [
            pltpu.roll(jnp.where(ahead, p, q), LANES + 1 - count, 1, stride=1, stride_axis=0)
            for p, q in zip(blocks, blocks[1:])
        ]
        store(vmid, vout, r + 2, first, (jnp.concatenate(turned, axis=1) * scale).astype(BF16))

    def flip(r, first, count):
        i = lax.broadcasted_iota(jnp.int32, (count, count), 0)
        j = lax.broadcasted_iota(jnp.int32, (count, count), 1)
        turn = jnp.where(i + j == count - 1, 1.0, 0.0).astype(BF16)
        pair = jnp.concatenate([rext[r + k, halo + first : halo + first + count, :] for k in range(2)], axis=1)
        piece = jnp.dot(turn, pair, preferred_element_type=F32).astype(BF16)
        at = width + E - first - count
        for k in range(2):
            rrev[r + k, at : at + count, :] = piece[:, k * chans : (k + 1) * chans]

    def tiles(cols):
        units = (cols[1] - cols[0]) // E
        n = -(-units * E // LANES)
        ends = [cols[0] + E * (units * k // n) for k in range(n + 1)]
        return [(p, q - p) for p, q in zip(ends, ends[1:])]

    def correlate_rows(seg, rs):
        for r in rs:
            for cols in vcols[seg]:
                for first, count in tiles(cols):
                    correlate(r, first, count)

    def flip_rows(cols, rs):
        for r in rs:
            for first, count in tiles(cols):
                flip(r, first, count)

    def send_rims(seg):
        start(has_u, rims[seg][0])
        start(has_d, rims[seg][1])

    def take_rims(seg):
        recv(has_d, rims[seg][0])
        recv(has_u, rims[seg][1])
        for l, h in vcols[seg]:
            for r in (0, 1, rows + 2, rows + 3):
                spread(vout, r, l, vmid[r, l + G : h + G, :])

    def gathered(mid_ref, out_ref, shift, parts):
        taps = [(out_ref, slice(0, disp)), (mid_ref, slice(0, disp)), (out_ref, slice(disp, 2 * disp))]
        return jnp.concatenate(
            [
                jnp.concatenate(
                    [
                        ref[pl.ds(g + a + shift, n), l + G : h + G, lanes].reshape(n * (h - l), disp)
                        for g, n, (l, h) in parts
                    ],
                    axis=0,
                )
                for a in range(3)
                for ref, lanes in taps
            ],
            axis=1,
        )

    def apart(body):
        @pl.loop(0, once)
        def _(_):
            body()

    def shares(parts):
        total = sum(n * (h - l) for _, n, (l, h) in parts)
        first, second, done = [], [], 0
        for g, n, (l, h) in parts:
            take = min(n, max(0, round((total / 2 - done) / (h - l))))
            if take:
                first.append((g, take, (l, h)))
                done += take * (h - l)
            if take < n:
                second.append((g + take, n - take, (l, h)))
        return [p for p in (first, second) if p]

    def conv1(parts):
        @apart
        def _():
            for share in shares(parts):
                conv1_share(share)

    def conv2(parts):
        @apart
        def _():
            for share in shares(parts):
                conv2_share(share)

    def conv1_share(parts):
        acc = jnp.dot(gathered(vmid, vout, 1, parts), w1[...], preferred_element_type=F32)
        at = 0
        for g, n, (l, h) in parts:
            size = h - l
            masked = l < 0 or h > width
            if masked:
                x = col * width + l + lax.broadcasted_iota(jnp.int32, (size, 1), 0)
                inside = (x >= 0) & (x < ncol * width)
            for r in range(g, g + n):
                value = jnp.maximum(acc[at : at + size], 0.0)
                if masked:
                    value = jnp.where(inside, value, 0.0)
                if r < 0 or r >= rows:
                    value = jnp.where(has_u if r < 0 else has_d, value, 0.0)
                store(hmid, hout, r + 1, l, value.astype(BF16))
                at += size

    def conv2_share(parts):
        acc = jnp.dot(gathered(hmid, hout, 0, parts), w2[...], preferred_element_type=F32)
        acc = jnp.maximum(acc, 0.0).astype(BF16)
        at = 0
        for g, n, (l, h) in parts:
            size = n * (h - l)
            out[pl.ds(g, n), l:h, :] = acc[at : at + size].reshape(n, h - l, disp)
            at += size

    def parts_of(groups, cols):
        return [(g, n, c) for g, n in groups for c in cols]

    def hid_inner(seg):
        return parts_of([(1, rows - 2)], hcols[seg])

    def hid_outer(seg):
        return parts_of([(-1, 2), (rows - 1, 2)], hcols[seg])

    def out_inner(seg):
        return parts_of([(2, rows - 4)], ocols[seg])

    def out_outer(seg):
        return parts_of([(0, 2), (rows - 2, 2)], ocols[seg])

    outer_rows = [0, 1, rows - 2, rows - 1]
    pairs = range(0, rows, 2)
    own[0].wait()

    flip_rows((0, width), pairs)

    pl.semaphore_wait(barrier, peers)
    start(has_l, edge_l)
    start(has_r, near + mid + edge_r + far + far_rest)

    own[1].wait()

    correlate_rows(SA, outer_rows)

    send_rims(SA)
    correlate_rows(SA, range(2, rows - 2))
    own[2].wait()
    conv1(hid_inner(SA))
    own[3].wait()
    conv2(out_inner(SA))

    recv(has_r, edge_l)
    recv(has_l, near)
    flip_rows((b2 - disp, 0), pairs)
    flip_rows((width, width + E), pairs)
    correlate_rows(SB, range(rows))
    send_rims(SB)
    take_rims(SA)
    conv1(hid_outer(SA) + hid_inner(SB))
    conv2(out_outer(SA) + out_inner(SB))

    recv(has_l, mid)
    flip_rows((b1 - disp, b2 - disp), pairs)
    correlate_rows(SC, range(rows))
    send_rims(SC)
    take_rims(SB)
    conv1(hid_outer(SB) + hid_inner(SC))
    conv2(out_outer(SB) + out_inner(SC))

    recv(has_l, edge_r + far)
    flip_rows((b0 - disp, b1 - disp), [0, rows - 2])
    correlate_rows(SD, outer_rows)
    send_rims(SD)
    recv(has_l, far_rest)
    flip_rows((b0 - disp, b1 - disp), range(2, rows - 2, 2))
    correlate_rows(SD, range(2, rows - 2))
    take_rims(SC)
    conv1(hid_outer(SC) + hid_inner(SD))
    conv2(out_outer(SC) + out_inner(SD))
    take_rims(SD)
    conv1(hid_outer(SD))
    conv2(out_outer(SD))

    sent(has_l, edge_l)
    sent(has_r, near + mid + edge_r + far + far_rest)
    for ups, downs in rims:
        sent(has_u, ups)
        sent(has_d, downs)


def local(ncol, nrow, left, right, w1, w2):
    rows, width, chans = left.shape
    disp = w1.shape[2]
    outs = w1.shape[3]
    w1 = w1.reshape(-1, outs)
    w2 = w2.reshape(-1, outs)
    span = width + disp + 2 * E + LANES
    wide = width + 2 * G
    hbm = pl.BlockSpec(memory_space=pl.ANY)
    copies = 18
    return pl.pallas_call(
        functools.partial(fixed, ncol, nrow),
        out_shape=pltpu.VMEM((rows, width, outs), BF16),
        in_specs=[hbm] * 4,
        out_specs=pl.BlockSpec(memory_space=pltpu.VMEM),
        scratch_shapes=[
            pltpu.VMEM((rows, width + disp + 2 * E, chans), BF16),
            pltpu.VMEM((rows, width + 2 * E, chans), BF16),
            pltpu.VMEM((rows, span, chans), BF16),
            pltpu.VMEM((rows + 4, wide, disp), BF16),
            pltpu.VMEM((rows + 4, wide, 2 * disp), BF16),
            pltpu.VMEM((rows + 2, wide, outs), BF16),
            pltpu.VMEM((rows + 2, wide, 2 * outs), BF16),
            pltpu.VMEM(w1.shape, BF16),
            pltpu.VMEM(w2.shape, BF16),
            pltpu.SemaphoreType.DMA((4,)),
            pltpu.SemaphoreType.DMA((copies,)),
            pltpu.SemaphoreType.DMA((copies,)),
        ],
        compiler_params=pltpu.CompilerParams(
            collective_id=0, has_side_effects=True, vmem_limit_bytes=67_043_328 - 2 * rows * width * outs - 2**18
        ),
    )(left, right, w1, w2)


def fixed(ncol, nrow, *refs):
    kernel(ncol, nrow, *refs)


def solution(mesh):
    in_specs = (P(("strip", "row"), "col", None), P(("strip", "row"), "col", None), P(), P())
    out_specs = P(("strip", "row"), "col", None)
    return jax.shard_map(
        functools.partial(local, mesh.shape["col"], mesh.shape["row"]),
        mesh=mesh, in_specs=in_specs, out_specs=out_specs, check_vma=False,
    )
```

```python
import functools

import jax
import jax.numpy as jnp
from jax import lax
from jax.experimental import pallas as pl
from jax.experimental.pallas import tpu as pltpu
from jax.sharding import PartitionSpec as P

MESH = pl.DeviceIdType.MESH
F32 = jnp.float32
BF16 = jnp.bfloat16
E = 16
G = 32
LANES = 128


def kernel(
    ncol, nrow, left, right, w1_hbm, w2_hbm, out,
    rext, lext, rrev, vmid, vout, hmid, hout, w1, w2, lsem, ssem, rsem,
):
    rows, width, chans = left.shape
    disp = w2_hbm.shape[1]
    col = lax.axis_index("col")
    row = lax.axis_index("row")
    has_l, has_r = col > 0, col < ncol - 1
    has_u, has_d = row > 0, row < nrow - 1
    to_l, to_r = {"col": col - 1}, {"col": col + 1}
    to_u, to_d = {"row": row - 1}, {"row": row + 1}
    halo = disp + E
    window = disp + LANES

    barrier = pltpu.get_barrier_semaphore()
    for has, to in ((has_l, to_l), (has_r, to_r), (has_u, to_u), (has_d, to_d)):
        @pl.when(has)
        def _():
            pl.semaphore_signal(barrier, inc=1, device_id=to, device_id_type=MESH)

    own = [
        pltpu.make_async_copy(right, rext.at[:, halo : halo + width], lsem.at[0]),
        pltpu.make_async_copy(left, lext.at[:, E : E + width], lsem.at[1]),
        pltpu.make_async_copy(w1_hbm, w1, lsem.at[2]),
        pltpu.make_async_copy(w2_hbm, w2, lsem.at[3]),
    ]
    for copy in own:
        copy.start()

    def clear(ref, *at):
        ref[at] = jnp.zeros(ref.at[at].shape, BF16)

    every = slice(0, rows)

    @pl.when(jnp.logical_not(has_l))
    def _():
        clear(rext, every, slice(0, halo))
        clear(lext, every, slice(0, E))

    @pl.when(jnp.logical_not(has_r))
    def _():
        clear(rext, every, slice(halo + width, halo + width + E))
        clear(lext, every, slice(E + width, 2 * E + width))

    @pl.when(jnp.logical_not(has_u))
    def _():
        clear(vmid, slice(0, 2))

    @pl.when(jnp.logical_not(has_d))
    def _():
        clear(vmid, slice(rows + 2, rows + 4))

    peers = sum(has.astype(jnp.int32) for has in (has_l, has_r, has_u, has_d))

    counter = [0]

    def remote(src, dst, to):
        at = counter[0]
        counter[0] += 1
        return pltpu.make_async_remote_copy(
            src_ref=src, dst_ref=dst, send_sem=ssem.at[at], recv_sem=rsem.at[at],
            device_id=to, device_id_type=MESH,
        )

    def start(has, copies):
        @pl.when(has)
        def _():
            for copy in copies:
                copy.start()

    def recv(has, copies):
        @pl.when(has)
        def _():
            for copy in copies:
                copy.wait_recv()

    def sent(has, copies):
        @pl.when(has)
        def _():
            for copy in copies:
                copy.wait_send()

    b0, b1, b2, b3, b4 = -E, 5 * E, 12 * E, disp, width - E
    vcols = [[(b3, b4)], [(b2, b3), (b4, width + E)], [(b1, b2)], [(b0, b1)]]
    hcols = [[(b3 + E, b4 - E)], [(b2 + E, b3 + E), (b4 - E, width + E)], [(b1 + E, b2 + E)], [(b0, b1 + E)]]
    ocols = [
        [(b3 + 2 * E, b4 - 2 * E)],
        [(b2 + 2 * E, b3 + 2 * E), (b4 - 2 * E, width)],
        [(b1 + 2 * E, b2 + 2 * E)],
        [(0, b1 + 2 * E)],
    ]
    SA, SB, SC, SD = range(4)

    def halo_part(first, last, r0, r1):
        return remote(
            right.at[r0:r1, width + first : width + last],
            rext.at[r0:r1, halo + first : halo + last], to_r,
        )

    edge_l = [
        remote(left.at[:, 0:E], lext.at[:, E + width : 2 * E + width], to_l),
        remote(right.at[:, 0:E], rext.at[:, halo + width : halo + width + E], to_l),
    ]
    near = [halo_part(b2 - disp, 0, 0, rows)]
    mid = [halo_part(b1 - disp, b2 - disp, 0, rows)]
    edge_r = [remote(left.at[:, width - E : width], lext.at[:, 0:E], to_r)]
    far = [halo_part(b0 - disp, b1 - disp, r, r + 2) for r in (0, rows - 2)]
    far_rest = [halo_part(b0 - disp, b1 - disp, 2, rows - 2)]

    def rim(cols):
        ups, downs = [], []
        for c in cols:
            at = slice(c[0] + G, c[1] + G)
            ups.append(remote(vmid.at[2:4, at], vmid.at[rows + 2 : rows + 4, at], to_u))
            downs.append(remote(vmid.at[rows : rows + 2, at], vmid.at[0:2, at], to_d))
        return ups, downs

    rims = [rim(c) for c in vcols]

    once = (col >= 0).astype(jnp.int32)
    scale = 1.0 / jnp.sqrt(F32(chans))

    def spread(out_ref, r, first, value):
        n = value.shape[0]
        for b in (0, 1):
            at = first + G + 1 - 2 * b
            out_ref[r, at : at + n, b * disp : (b + 1) * disp] = value

    def store(mid_ref, out_ref, r, first, value):
        mid_ref[r, first + G : first + G + value.shape[0], :] = value
        spread(out_ref, r, first, value)

    def correlate(r, first, count):
        at = width + E - first - count
        scores = lax.dot_general(
            lext[r, first + E : first + E + count, :],
            rrev[r, at : at + window, :],
            (((1,), (1,)), ((), ())),
            preferred_element_type=F32,
        )
        i = lax.broadcasted_iota(jnp.int32, (count, LANES), 0)
        j = lax.broadcasted_iota(jnp.int32, (count, LANES), 1)
        ahead = i + j >= count - 1
        blocks = [scores[:, k : k + LANES] for k in range(0, window, LANES)]
        turned = [
            pltpu.roll(jnp.where(ahead, p, q), LANES + 1 - count, 1, stride=1, stride_axis=0)
            for p, q in zip(blocks, blocks[1:])
        ]
        store(vmid, vout, r + 2, first, (jnp.concatenate(turned, axis=1) * scale).astype(BF16))

    def flip(r, first, count):
        i = lax.broadcasted_iota(jnp.int32, (count, count), 0)
        j = lax.broadcasted_iota(jnp.int32, (count, count), 1)
        turn = jnp.where(i + j == count - 1, 1.0, 0.0).astype(BF16)
        pair = jnp.concatenate([rext[r + k, halo + first : halo + first + count, :] for k in range(2)], axis=1)
        piece = jnp.dot(turn, pair, preferred_element_type=F32).astype(BF16)
        at = width + E - first - count
        for k in range(2):
            rrev[r + k, at : at + count, :] = piece[:, k * chans : (k + 1) * chans]

    def tiles(cols):
        units = (cols[1] - cols[0]) // E
        n = -(-units * E // LANES)
        ends = [cols[0] + E * (units * k // n) for k in range(n + 1)]
        return [(p, q - p) for p, q in zip(ends, ends[1:])]

    def correlate_rows(seg, rs):
        for r in rs:
            for cols in vcols[seg]:
                for first, count in tiles(cols):
                    correlate(r, first, count)

    def flip_rows(cols, rs):
        for r in rs:
            for first, count in tiles(cols):
                flip(r, first, count)

    def send_rims(seg):
        start(has_u, rims[seg][0])
        start(has_d, rims[seg][1])

    def take_rims(seg):
        recv(has_d, rims[seg][0])
        recv(has_u, rims[seg][1])
        for l, h in vcols[seg]:
            for r in (0, 1, rows + 2, rows + 3):
                spread(vout, r, l, vmid[r, l + G : h + G, :])

    def gathered(mid_ref, out_ref, shift, parts):
        taps = [(out_ref, slice(0, disp)), (mid_ref, slice(0, disp)), (out_ref, slice(disp, 2 * disp))]
        return jnp.concatenate(
            [
                jnp.concatenate(
                    [
                        ref[pl.ds(g + a + shift, n), l + G : h + G, lanes].reshape(n * (h - l), disp)
                        for g, n, (l, h) in parts
                    ],
                    axis=0,
                )
                for a in range(3)
                for ref, lanes in taps
            ],
            axis=1,
        )

    def apart(body):
        @pl.loop(0, once)
        def _(_):
            body()

    def shares(parts):
        total = sum(n * (h - l) for _, n, (l, h) in parts)
        first, second, done = [], [], 0
        for g, n, (l, h) in parts:
            take = min(n, max(0, round((total / 2 - done) / (h - l))))
            if take:
                first.append((g, take, (l, h)))
                done += take * (h - l)
            if take < n:
                second.append((g + take, n - take, (l, h)))
        return [p for p in (first, second) if p]

    def conv1(parts):
        @apart
        def _():
            for share in shares(parts):
                conv1_share(share)

    def conv2(parts):
        @apart
        def _():
            for share in shares(parts):
                conv2_share(share)

    def conv1_share(parts):
        acc = jnp.dot(gathered(vmid, vout, 1, parts), w1[...], preferred_element_type=F32)
        at = 0
        for g, n, (l, h) in parts:
            size = h - l
            masked = l < 0 or h > width
            if masked:
                x = col * width + l + lax.broadcasted_iota(jnp.int32, (size, 1), 0)
                inside = (x >= 0) & (x < ncol * width)
            for r in range(g, g + n):
                value = jnp.maximum(acc[at : at + size], 0.0)
                if masked:
                    value = jnp.where(inside, value, 0.0)
                if r < 0 or r >= rows:
                    value = jnp.where(has_u if r < 0 else has_d, value, 0.0)
                store(hmid, hout, r + 1, l, value.astype(BF16))
                at += size

    def conv2_share(parts):
        acc = jnp.dot(gathered(hmid, hout, 0, parts), w2[...], preferred_element_type=F32)
        acc = jnp.maximum(acc, 0.0).astype(BF16)
        at = 0
        for g, n, (l, h) in parts:
            size = n * (h - l)
            out[pl.ds(g, n), l:h, :] = acc[at : at + size].reshape(n, h - l, disp)
            at += size

    def parts_of(groups, cols):
        return [(g, n, c) for g, n in groups for c in cols]

    def hid_inner(seg):
        return parts_of([(1, rows - 2)], hcols[seg])

    def hid_outer(seg):
        return parts_of([(-1, 2), (rows - 1, 2)], hcols[seg])

    def out_inner(seg):
        return parts_of([(2, rows - 4)], ocols[seg])

    def out_outer(seg):
        return parts_of([(0, 2), (rows - 2, 2)], ocols[seg])

    outer_rows = [0, 1, rows - 2, rows - 1]
    pairs = range(0, rows, 2)
    own[0].wait()

    flip_rows((0, width), pairs)

    pl.semaphore_wait(barrier, peers)
    start(has_l, edge_l)
    start(has_r, near + mid + edge_r + far + far_rest)

    own[1].wait()

    correlate_rows(SA, outer_rows)

    send_rims(SA)
    correlate_rows(SA, range(2, rows - 2))
    own[2].wait()
    conv1(hid_inner(SA))
    own[3].wait()
    conv2(out_inner(SA))

    recv(has_r, edge_l)
    recv(has_l, near)
    flip_rows((b2 - disp, 0), pairs)
    flip_rows((width, width + E), pairs)
    correlate_rows(SB, range(rows))
    send_rims(SB)
    take_rims(SA)
    conv1(hid_outer(SA) + hid_inner(SB))
    conv2(out_outer(SA) + out_inner(SB))

    recv(has_l, mid)
    flip_rows((b1 - disp, b2 - disp), pairs)
    correlate_rows(SC, range(rows))
    send_rims(SC)
    take_rims(SB)
    conv1(hid_outer(SB) + hid_inner(SC))
    conv2(out_outer(SB) + out_inner(SC))

    recv(has_l, edge_r + far)
    flip_rows((b0 - disp, b1 - disp), [0, rows - 2])
    correlate_rows(SD, outer_rows)
    send_rims(SD)
    recv(has_l, far_rest)
    flip_rows((b0 - disp, b1 - disp), range(2, rows - 2, 2))
    correlate_rows(SD, range(2, rows - 2))
    take_rims(SC)
    conv1(hid_outer(SC) + hid_inner(SD))
    conv2(out_outer(SC) + out_inner(SD))
    take_rims(SD)
    conv1(hid_outer(SD))
    conv2(out_outer(SD))

    sent(has_l, edge_l)
    sent(has_r, near + mid + edge_r + far + far_rest)
    for ups, downs in rims:
        sent(has_u, ups)
        sent(has_d, downs)


def local(ncol, nrow, left, right, w1, w2):
    rows, width, chans = left.shape
    disp = w1.shape[2]
    outs = w1.shape[3]
    w1 = w1.reshape(-1, outs)
    w2 = w2.reshape(-1, outs)
    span = width + disp + 2 * E + LANES
    wide = width + 2 * G
    hbm = pl.BlockSpec(memory_space=pl.ANY)
    copies = 18
    return pl.pallas_call(
        functools.partial(fixed, ncol, nrow),
        out_shape=pltpu.VMEM((rows, width, outs), BF16),
        in_specs=[hbm] * 4,
        out_specs=pl.BlockSpec(memory_space=pltpu.VMEM),
        scratch_shapes=[
            pltpu.VMEM((rows, width + disp + 2 * E, chans), BF16),
            pltpu.VMEM((rows, width + 2 * E, chans), BF16),
            pltpu.VMEM((rows, span, chans), BF16),
            pltpu.VMEM((rows + 4, wide, disp), BF16),
            pltpu.VMEM((rows + 4, wide, 2 * disp), BF16),
            pltpu.VMEM((rows + 2, wide, outs), BF16),
            pltpu.VMEM((rows + 2, wide, 2 * outs), BF16),
            pltpu.VMEM(w1.shape, BF16),
            pltpu.VMEM(w2.shape, BF16),
            pltpu.SemaphoreType.DMA((4,)),
            pltpu.SemaphoreType.DMA((copies,)),
            pltpu.SemaphoreType.DMA((copies,)),
        ],
        compiler_params=pltpu.CompilerParams(
            collective_id=0, has_side_effects=True, vmem_limit_bytes=67_043_328 - 2 * rows * width * outs - 2**18
        ),
    )(left, right, w1, w2)


def fixed(ncol, nrow, *refs):
    kernel(ncol, nrow, *refs)


def solution(mesh):
    in_specs = (P(("strip", "row"), "col", None), P(("strip", "row"), "col", None), P(), P())
    out_specs = P(("strip", "row"), "col", None)
    return jax.shard_map(
        functools.partial(local, mesh.shape["col"], mesh.shape["row"]),
        mesh=mesh, in_specs=in_specs, out_specs=out_specs, check_vma=False,
    )
```
